32 devices in a mesh: parts: 2 (over y), tm: 16 (over z, x, core).
Axes of the slice: x: 2, y: 2, z: 4, core: 2. Of those that a mesh axis runs over, the one named last changes fastest.
Arguments:
- signal: bfloat16 [16384, 1024], P(('parts', 'tm')), parts along dimension 0, may hold values from -6 to 6
- pool_weight: bfloat16 [4096, 2048], P('tm'), may hold values from -0.09375 to 0.09375
- norm_gain: float32 [2, 2048], replicated, may hold values from 0.1 to 1.9
- step_size: float32 [2, 2048], replicated, may hold values from 0 to 0.05, as said below
- mode_out: float32 [2, 32, 2048], replicated, may hold values from -1 to 1
- skip_gain: float32 [2, 2048], replicated, may hold values from -4 to 4
Outputs:
- pooled_out: bfloat16 [4096, 2048], P(('parts', 'tm')), parts along dimension 0
The draws below stay inside these ranges and needn't reach their ends.
There are 2 independent parts, one for each index of `parts`. The reference program is written for one: setup_inputs(seed, part) draws one part's arguments, and reference() takes and returns one part's arrays. A program takes and returns all parts, laid end to end along the dimension named above; an argument that names none is the same for every part. Nothing has to cross between parts.
Inputs may be any that keep to these rules, and one draw needn't show every extreme that they name: `step_size`: positive step sizes.
All inputs are finite; a program needn't handle non-finite values.
Results may differ from the reference program's by a relative error of at most 0.001.
Values may be sent and summed in bfloat16 or wider, within the bound.
A program may use at most 320 MiB of HBM per device.

```python
import jax
import jax.numpy as jnp
from jax import lax

CIN = 1024
H = 2048
NS = 32
POOL = 4
LAYERS = 2
SEQ = 2048
FINE = 8192


def draw_step_size(key, part):
    pick_key, slow_key, fast_key = jax.random.split(key, 3)
    slow_share = 0.5
    slow_low = 0.3
    slow_high = 3.0
    slow_pick = jax.random.bernoulli(pick_key, slow_share, (LAYERS, H))
    slow_steps = jnp.exp(jax.random.uniform(slow_key, (LAYERS, H), jnp.float32, jnp.log(slow_low), jnp.log(slow_high))) / SEQ
    fast_steps = jnp.exp(jax.random.uniform(fast_key, (LAYERS, H), jnp.float32, jnp.log(1.0 / 48.0), jnp.log(1.0 / 24.0)))
    return jnp.where(slow_pick, slow_steps, fast_steps).astype(jnp.float32)


def level_of(own_key, dims, cuts, least, largest):
    def one(axis_at, blocks):
        heights = jax.random.uniform(jax.random.fold_in(jax.random.fold_in(own_key, 6), axis_at), (blocks,), jnp.float32, least / len(cuts), largest / len(cuts))
        return jnp.repeat(jnp.exp(heights), dims[axis_at] // blocks).reshape((-1,) + (1,) * (len(dims) - axis_at - 1))

    gain = one(*cuts[0])
    for cut in cuts[1:]:
        gain = gain * one(*cut)
    return gain


def bell_draw(own_key, dims, deviation, bound, cuts=(), held_as=jnp.bfloat16):
    gain = level_of(own_key, dims, cuts, -0.22, 0.18) if cuts else 1.0
    entries = jax.random.normal(own_key, dims, jnp.float32) * deviation * gain
    return jnp.minimum(jnp.maximum(entries, -bound), bound).astype(held_as)


def setup_inputs(seed: int = 0, part: int = 0) -> dict:
    splits = jax.random.split(jax.random.key(seed), 7)
    part_splits = jax.random.split(jax.random.fold_in(splits[6], part), 7)
    signal = bell_draw(part_splits[0], (FINE, CIN), 1.0, 6.0, ((0, 16),))
    pool_weight = bell_draw(splits[1], (POOL * CIN, H), (POOL * CIN) ** -0.5, 0.09375, ((0, 16),))
    norm_gain = jnp.clip(1.0 + 0.18 * jax.random.normal(splits[2], (LAYERS, H), jnp.float32), 0.1, 1.9)
    step_size = draw_step_size(jax.random.fold_in(splits[6], 71), part)
    mode_out = bell_draw(splits[4], (LAYERS, NS, H), NS ** -0.5, 1.0, (), jnp.float32)
    skip_gain = bell_draw(splits[5], (LAYERS, H), 1.0, 4.0, (), jnp.float32)
    return {"signal": signal, "pool_weight": pool_weight, "norm_gain": norm_gain, "step_size": step_size, "mode_out": mode_out, "skip_gain": skip_gain}


def build_tables(decay_rates, in_scale, out_mix, block_len):
    lag_steps = jnp.arange(block_len, dtype=jnp.float32)
    powers = jnp.exp(-lag_steps[:, None, None] * decay_rates[None])
    kernel = lax.optimization_barrier(jnp.sum(out_mix[None] * in_scale[None] * powers, axis=1))
    lag_index = jnp.arange(block_len, dtype=jnp.int32)
    lag_gap = lag_index[:, None] - lag_index[None, :]
    picked = kernel[jnp.clip(lag_gap, 0, block_len - 1).astype(jnp.int32)]
    toeplitz = jnp.where((lag_gap >= 0)[:, :, None], picked, jnp.zeros_like(picked))
    into_table = in_scale[None] * jnp.exp(-(block_len - 1 - lag_steps)[:, None, None] * decay_rates[None])
    outof_table = out_mix[None] * jnp.exp(-(lag_steps + 1.0)[:, None, None] * decay_rates[None])
    return (toeplitz, into_table, outof_table)

def layer_norm(hidden, gain_row):
    row_mean = lax.optimization_barrier(jnp.mean(hidden, axis=-1, keepdims=True))
    centered = hidden - row_mean
    row_var = lax.optimization_barrier(jnp.mean(centered * centered, axis=-1, keepdims=True))
    return centered * lax.rsqrt(row_var + 1e-05) * gain_row[None, :]

def state_layer(hidden, gain_row, step_row, out_mix, skip_row):
    row_count, chan_count = hidden.shape
    modes = out_mix.shape[0]
    block_len = min(64, row_count)
    blocks = row_count // block_len
    normed = layer_norm(hidden, gain_row)
    decay_rates = step_row[None, :] * (jnp.arange(modes, dtype=jnp.float32) + 1.0)[:, None]
    in_scale = jnp.sqrt(-jnp.expm1(-2.0 * decay_rates))
    toeplitz, into_table, outof_table = build_tables(decay_rates, in_scale, out_mix, block_len)
    block_decay = jnp.exp(-decay_rates * block_len)
    exact = lax.Precision.HIGHEST
    grouped = normed.reshape(blocks, block_len, chan_count)

    def advance(state, block_rows):
        inner = jnp.einsum('tsh,sh->th', toeplitz, block_rows, precision=exact)
        carried = jnp.einsum('tnh,nh->th', outof_table, state, precision=exact)
        response = inner + carried + skip_row[None, :] * block_rows
        new_state = block_decay * state + jnp.einsum('snh,sh->nh', into_table, block_rows, precision=exact)
        return (new_state, response)
    start_state = jnp.zeros((modes, chan_count), jnp.float32)
    final_state, responses = lax.scan(advance, start_state, grouped)
    response = responses.reshape(row_count, chan_count)
    return hidden + jax.nn.gelu(response, approximate=False)

def reference(signal, pool_weight, norm_gain, step_size, mode_out, skip_gain):
    coarse = signal.reshape(SEQ, POOL * CIN)
    hidden = jnp.dot(coarse, pool_weight, preferred_element_type=jnp.float32)
    for layer_index in range(LAYERS):
        hidden = state_layer(hidden, norm_gain[layer_index], step_size[layer_index], mode_out[layer_index], skip_gain[layer_index])
    return hidden.astype(jnp.bfloat16)
```

```python
import functools

import jax
import jax.numpy as jnp
from jax import lax
from jax.experimental import pallas as pl
from jax.experimental.pallas import tpu as pltpu
from jax.sharding import PartitionSpec as P

POOL = 4
SPLIT = 4
BLOCK = 16
LANES = 128


def block_ends(x_ref, decay_ref, ends_ref, modes, cols):
    rows = x_ref.shape[0]
    blocks = rows // BLOCK
    span = 8 * BLOCK

    def group(g, carry):
        base = pl.multiple_of(g * span, span)
        xs = [x_ref[pl.ds(base + j, 8, stride=BLOCK), cols] for j in range(BLOCK)]
        for n in range(modes):
            decay = jnp.broadcast_to(decay_ref[pl.ds(n, 1), cols], (8, LANES))
            end = xs[0]
            for j in range(1, BLOCK):
                end = end * decay + xs[j]
            ends_ref[pl.ds(pl.multiple_of(n * blocks + g * 8, 8), 8), cols] = end
        return carry

    lax.fori_loop(0, rows // span, group, 0)


def scan_blocks(ends_ref, step_ref, modes, cols, start, out_ref=None):
    blocks = ends_ref.shape[0] // modes
    groups = modes // 8
    steps = [step_ref[pl.ds(i * 8, 8), cols] for i in range(groups)]
    outs = [out_ref[pl.ds(i * 8, 8), cols] for i in range(groups)] if out_ref is not None else None
    states = list(start)
    for b in range(blocks):
        for i in range(groups):
            where = pl.ds(i * 8 * blocks + b, 8, stride=blocks)
            end = ends_ref[where, cols]
            if outs is not None:
                ends_ref[where, cols] = states[i] * outs[i]
            states[i] = states[i] * steps[i] + end
    return states


def respond(x_ref, hidden_ref, ends_ref, powers_ref, kernel_ref, result_ref, modes, cols):
    rows = x_ref.shape[0]
    blocks = rows // BLOCK
    span = 8 * BLOCK

    def group(g, carry):
        base = pl.multiple_of(g * span, span)
        coefs = [
            ends_ref[pl.ds(pl.multiple_of(n * blocks + g * 8, 8), 8), cols] for n in range(modes)
        ]
        xs = [x_ref[pl.ds(base + j, 8, stride=BLOCK), cols] for j in range(BLOCK)]
        for j in range(BLOCK):
            power = jnp.broadcast_to(powers_ref[pl.ds(j, 1), cols], (8, LANES))
            total = coefs[modes - 1]
            for n in range(modes - 2, -1, -1):
                total = total * power + coefs[n]
            total = total * power
            for i in range(j + 1):
                total = total + xs[i] * jnp.broadcast_to(
                    kernel_ref[pl.ds(j - i, 1), cols], (8, LANES)
                )
            where = pl.ds(base + j, 8, stride=BLOCK)
            gelu = 0.5 * total * (1.0 + lax.erf(total * 0.7071067811865476))
            result_ref[where, cols] = hidden_ref[where, cols] + gelu
        return carry

    lax.fori_loop(0, rows // span, group, 0)


def ends_kernel(modes, x_ref, decay_ref, step_ref, ends_ref, last_ref):
    cols = slice(None)
    block_ends(x_ref, decay_ref, ends_ref, modes, cols)
    zero = [jnp.zeros((8, LANES), jnp.float32)] * (modes // 8)
    last = scan_blocks(ends_ref, step_ref, modes, cols, zero)
    for i in range(modes // 8):
        last_ref[pl.ds(i * 8, 8), cols] = last[i]


def respond_kernel(
    modes, x_ref, hidden_ref, ends_in_ref, start_ref, step_ref, out_ref, powers_ref, kernel_ref,
    result_ref, ends_ref
):
    cols = slice(None)
    ends_ref[...] = ends_in_ref[...]
    start = [start_ref[pl.ds(i * 8, 8), cols] for i in range(modes // 8)]
    scan_blocks(ends_ref, step_ref, modes, cols, start, out_ref)
    respond(x_ref, hidden_ref, ends_ref, powers_ref, kernel_ref, result_ref, modes, cols)


def by_lanes(rows):
    return pl.BlockSpec((rows, LANES), lambda i: (0, i))


def tables(step_row, out_mix, skip_row, rows):
    modes = out_mix.shape[0]
    rates = step_row[None, :] * (jnp.arange(modes, dtype=jnp.float32) + 1.0)[:, None]
    in_scale = jnp.sqrt(-jnp.expm1(-2.0 * rates))
    out = out_mix * in_scale
    lags = jnp.arange(BLOCK, dtype=jnp.float32)
    kernel = jnp.sum(out[None] * jnp.exp(-lags[:, None, None] * rates[None]), axis=1)
    kernel = kernel.at[0].add(skip_row)
    powers = jnp.exp(-(lags + 1.0)[:, None] * step_row[None, :])
    return {
        "decay": jnp.exp(-rates),
        "step": jnp.exp(-rates * BLOCK),
        "whole": jnp.exp(-rates * rows),
        "out": out,
        "powers": powers,
        "kernel": kernel,
    }


def state_layer(hidden, gain, table, low_groups, high_groups):
    rows, chans = hidden.shape
    modes = table["decay"].shape[0]
    blocks = rows // BLOCK
    mean = jnp.mean(hidden, axis=-1)
    spread = jnp.sum(jnp.square(hidden - mean[:, None]), axis=-1)
    stats = lax.all_gather(jnp.stack([mean, spread]), "tm", axis_index_groups=low_groups)
    row_mean = jnp.mean(stats[:, 0], axis=0)
    row_var = (
        jnp.sum(stats[:, 1], axis=0) + chans * jnp.sum(jnp.square(stats[:, 0] - row_mean), axis=0)
    ) / (chans * SPLIT)
    normed = (hidden - row_mean[:, None]) * lax.rsqrt(row_var + 1e-05)[:, None] * gain[None, :]
    grid = (chans // LANES,)
    ends, last = pl.pallas_call(
        functools.partial(ends_kernel, modes),
        grid=grid,
        in_specs=[by_lanes(rows), by_lanes(modes), by_lanes(modes)],
        out_specs=[by_lanes(modes * blocks), by_lanes(modes)],
        out_shape=[
            jax.ShapeDtypeStruct((modes * blocks, chans), jnp.float32),
            jax.ShapeDtypeStruct((modes, chans), jnp.float32),
        ],
    )(normed, table["decay"], table["step"])
    every = lax.all_gather(last, "tm", axis_index_groups=high_groups)
    mine = lax.axis_index("tm") // SPLIT
    start = jnp.zeros_like(last)
    for p in range(len(high_groups[0]) - 1):
        start = jnp.where(p < mine, table["whole"] * start + every[p], start)
    return pl.pallas_call(
        functools.partial(respond_kernel, modes),
        grid=grid,
        in_specs=[
            by_lanes(rows), by_lanes(rows), by_lanes(modes * blocks), by_lanes(modes),
            by_lanes(modes), by_lanes(modes), by_lanes(BLOCK), by_lanes(BLOCK),
        ],
        out_specs=by_lanes(rows),
        out_shape=jax.ShapeDtypeStruct((rows, chans), jnp.float32),
        scratch_shapes=[pltpu.VMEM((modes * blocks, LANES), jnp.float32)],
    )(normed, hidden, ends, start, table["step"], table["out"], table["powers"], table["kernel"])


def local(signal, pool_weight, norm_gain, step_size, mode_out, skip_gain):
    fine_rows, channels = signal.shape
    count = lax.axis_size("tm")
    low = lax.axis_index("tm") % SPLIT
    low_groups = [[h * SPLIT + i for i in range(SPLIT)] for h in range(count // SPLIT)]
    high_groups = [[h * SPLIT + i for h in range(count // SPLIT)] for i in range(SPLIT)]
    coarse = signal.reshape(fine_rows // POOL, POOL * channels)
    coarse = lax.all_gather(coarse, "tm", axis_index_groups=low_groups, axis=0, tiled=True)
    weight = lax.all_to_all(
        pool_weight, "tm", 1, 0, axis_index_groups=low_groups, tiled=True
    )
    weight = lax.all_gather(weight, "tm", axis_index_groups=high_groups, axis=0, tiled=True)
    hidden = jnp.dot(coarse, weight, preferred_element_type=jnp.float32)
    rows, chans = hidden.shape

    def own(array):
        return lax.dynamic_slice_in_dim(array, low * chans, chans, axis=array.ndim - 1)

    gain, step, mix, skip = own(norm_gain), own(step_size), own(mode_out), own(skip_gain)
    for l in range(norm_gain.shape[0]):
        table = tables(step[l], mix[l], skip[l], rows)
        hidden = state_layer(hidden, gain[l], table, low_groups, high_groups)
    return lax.all_to_all(
        hidden.astype(jnp.bfloat16), "tm", 0, 1, axis_index_groups=low_groups, tiled=True
    )


def solution(mesh):
    placed = (P(("parts", "tm"), None), P("tm", None), P(), P(), P(), P())
    return jax.shard_map(
        local, mesh=mesh, in_specs=placed, out_specs=P(("parts", "tm"), None), check_vma=False
    )
```

```python
import functools

import jax
import jax.numpy as jnp
from jax import lax
from jax.experimental import pallas as pl
from jax.experimental.pallas import tpu as pltpu
from jax.sharding import PartitionSpec as P

POOL = 4
SPLIT = 4
BLOCK = 16
LANES = 128
PIECES = 4


def block_ends(x_ref, decay_ref, ends_ref, modes, cols):
    rows = x_ref.shape[0]
    blocks = rows // BLOCK
    span = 8 * BLOCK

    def group(g, carry):
        base = pl.multiple_of(g * span, span)
        xs = [x_ref[pl.ds(base + j, 8, stride=BLOCK), cols] for j in range(BLOCK)]
        for n in range(modes):
            decay = jnp.broadcast_to(decay_ref[pl.ds(n, 1), cols], (8, LANES))
            end = xs[0]
            for j in range(1, BLOCK):
                end = end * decay + xs[j]
            ends_ref[pl.ds(pl.multiple_of(n * blocks + g * 8, 8), 8), cols] = end
        return carry

    lax.fori_loop(0, rows // span, group, 0)


def scan_blocks(ends_ref, step_ref, modes, cols, start, out_ref=None):
    blocks = ends_ref.shape[0] // modes
    groups = modes // 8
    steps = [step_ref[pl.ds(i * 8, 8), cols] for i in range(groups)]
    outs = [out_ref[pl.ds(i * 8, 8), cols] for i in range(groups)] if out_ref is not None else None
    states = list(start)
    for b in range(blocks):
        for i in range(groups):
            where = pl.ds(i * 8 * blocks + b, 8, stride=blocks)
            end = ends_ref[where, cols]
            if outs is not None:
                ends_ref[where, cols] = states[i] * outs[i]
            states[i] = states[i] * steps[i] + end
    return states


def respond(x_ref, hidden_ref, ends_ref, powers_ref, kernel_ref, result_ref, modes, cols):
    rows = x_ref.shape[0]
    blocks = rows // BLOCK
    span = 8 * BLOCK

    def group(g, carry):
        base = pl.multiple_of(g * span, span)
        coefs = [
            ends_ref[pl.ds(pl.multiple_of(n * blocks + g * 8, 8), 8), cols] for n in range(modes)
        ]
        xs = [x_ref[pl.ds(base + j, 8, stride=BLOCK), cols] for j in range(BLOCK)]
        for j in range(BLOCK):
            power = jnp.broadcast_to(powers_ref[pl.ds(j, 1), cols], (8, LANES))
            total = coefs[modes - 1]
            for n in range(modes - 2, -1, -1):
                total = total * power + coefs[n]
            total = total * power
            for i in range(j + 1):
                total = total + xs[i] * jnp.broadcast_to(
                    kernel_ref[pl.ds(j - i, 1), cols], (8, LANES)
                )
            where = pl.ds(base + j, 8, stride=BLOCK)
            gelu = 0.5 * total * (1.0 + lax.erf(total * 0.7071067811865476))
            result_ref[where, cols] = hidden_ref[where, cols] + gelu
        return carry

    lax.fori_loop(0, rows // span, group, 0)


def ends_kernel(modes, x_ref, decay_ref, step_ref, ends_ref, last_ref):
    cols = slice(None)
    block_ends(x_ref, decay_ref, ends_ref, modes, cols)
    zero = [jnp.zeros((8, LANES), jnp.float32)] * (modes // 8)
    last = scan_blocks(ends_ref, step_ref, modes, cols, zero)
    for i in range(modes // 8):
        last_ref[pl.ds(i * 8, 8), cols] = last[i]


def respond_kernel(
    modes, x_ref, hidden_ref, ends_in_ref, start_ref, step_ref, out_ref, powers_ref, kernel_ref,
    result_ref, ends_ref
):
    cols = slice(None)
    ends_ref[...] = ends_in_ref[...]
    start = [start_ref[pl.ds(i * 8, 8), cols] for i in range(modes // 8)]
    scan_blocks(ends_ref, step_ref, modes, cols, start, out_ref)
    respond(x_ref, hidden_ref, ends_ref, powers_ref, kernel_ref, result_ref, modes, cols)


MESH = pl.DeviceIdType.MESH


def pool_kernel(highs, coarse_ref, weight_ref, hidden_ref, all_ref, cols_ref, sems):
    part, place = lax.axis_index("parts"), lax.axis_index("tm")
    high, low = place // SPLIT, place % SPLIT
    depth, width = weight_ref.shape[0], cols_ref.shape[1]
    half = depth // 2
    rows = coarse_ref.shape[0]
    piece = rows // PIECES
    chunk = SPLIT * depth
    other = 1 - part
    (near_send, near_recv, own_sem, line_send, line_recv, side_send, side_recv,
     rows_send, rows_recv) = sems
    flip = lambda bit: low + bit - 2 * bit * ((low // bit) % 2)
    core, cross = flip(1), flip(2)
    diagonal = SPLIT - 1 - low
    at = lambda p, h, l: (p, h * SPLIT + l)

    barrier = pltpu.get_barrier_semaphore()

    def greet(device):
        pl.semaphore_signal(barrier, inc=1, device_id=device, device_id_type=MESH)

    for who in (core, cross, diagonal):
        greet(at(part, high, who))
    greet(at(other, high, low))
    pl.when(high > 0)(lambda: greet(at(part, high - 1, low)))
    pl.when(high < highs - 1)(lambda: greet(at(part, high + 1, low)))

    def spot(h, l, which):
        start = pl.multiple_of(h * chunk + l * depth + which * half, half)
        return cols_ref.at[pl.ds(start, half), :]

    def near(bit, which):
        to = (core, cross, diagonal)[bit]
        mine = weight_ref.at[
            pl.ds(pl.multiple_of(which * half, half), half),
            pl.ds(pl.multiple_of(to * width, width), width),
        ]
        return pltpu.make_async_remote_copy(
            mine, spot(high, low, which), near_send.at[bit, which], near_recv.at[bit, which],
            device_id=at(part, high, to), device_id_type=MESH,
        )

    def near_arrived(bit, which):
        who = (core, cross, diagonal)[bit]
        pltpu.make_async_remote_copy(
            spot(high, who, which), spot(high, who, which), near_send.at[bit, which],
            near_recv.at[bit, which], device_id=at(part, high, who), device_id_type=MESH,
        ).wait_recv()

    def line(up, h, l):
        to = jnp.clip(high + (1 if up else -1), 0, highs - 1)
        return pltpu.make_async_remote_copy(
            spot(h, l, part), spot(h, l, part), line_send.at[int(up), h, l], line_recv.at[h, l],
            device_id=at(part, to, low), device_id_type=MESH,
        )

    def side(h, l, which):
        return pltpu.make_async_remote_copy(
            spot(h, l, which), spot(h, l, which), side_send.at[h, l], side_recv.at[h, l],
            device_id=at(other, high, low), device_id_type=MESH,
        )

    def block(owner, p):
        start = pl.multiple_of(owner * rows + p * piece, piece)
        return all_ref.at[pl.ds(start, piece), :]

    def give(bit, p):
        to = core if bit == 0 else cross
        return pltpu.make_async_remote_copy(
            coarse_ref.at[pl.ds(p * piece, piece), :], block(low, p), rows_send.at[bit, p],
            rows_recv.at[bit, p], device_id=at(part, high, to), device_id_type=MESH,
        )

    def taken(bit, p):
        who = (core, cross, diagonal)[bit]
        pltpu.make_async_remote_copy(
            block(who, p), block(who, p), rows_send.at[bit, p], rows_recv.at[bit, p],
            device_id=at(part, high, core), device_id_type=MESH,
        ).wait_recv()

    def pass_on(p):
        return pltpu.make_async_remote_copy(
            block(cross, p), block(cross, p), rows_send.at[2, p], rows_recv.at[2, p],
            device_id=at(part, high, core), device_id_type=MESH,
        )

    own_weight = pltpu.make_async_copy(
        weight_ref.at[:, pl.ds(pl.multiple_of(low * width, width), width)],
        cols_ref.at[pl.ds(pl.multiple_of(high * chunk + low * depth, depth), depth), :],
        own_sem.at[0],
    )
    own_rows = pltpu.make_async_copy(
        coarse_ref, all_ref.at[pl.ds(pl.multiple_of(low * rows, rows), rows), :], own_sem.at[1]
    )
    own_weight.start()
    own_rows.start()
    ahead = jnp.minimum(high, 1) + jnp.minimum(highs - 1 - high, 1)
    pl.semaphore_wait(barrier, 4 + ahead)

    for bit in (1, 2, 0):
        near(bit, part).start()
    for p in range(PIECES):
        give(1, p).start()
    for p in range(PIECES):
        give(0, p).start()
    for bit in (1, 2, 0):
        near(bit, other).start()

    def both_ways(h, l):
        pl.when(high < highs - 1)(lambda: line(True, h, l).start())
        pl.when(high > 0)(lambda: line(False, h, l).start())

    own_weight.wait()
    both_ways(high, low)
    for bit, who in ((0, core), (1, cross), (2, diagonal)):
        near_arrived(bit, part)
        both_ways(high, who)

    def step(s, carry):
        for l in range(SPLIT):
            @pl.when(high - s >= 0)
            def _():
                h = high - s
                line(True, h, l).wait_recv()
                pl.when(high < highs - 1)(lambda: line(True, h, l).start())
                side(h, l, part).start()

            @pl.when(high + s < highs)
            def _():
                h = high + s
                line(False, h, l).wait_recv()
                pl.when(high > 0)(lambda: line(False, h, l).start())
                side(h, l, part).start()

        @pl.when(s < PIECES)
        def _():
            taken(1, s - 1)
            pass_on(s - 1).start()

        return carry

    lax.fori_loop(1, highs, step, 0)
    for p in range(min(PIECES - 1, highs - 1), PIECES):
        taken(1, p)
        pass_on(p).start()
    own_rows.wait()
    for p in range(PIECES):
        taken(0, p)
        taken(2, p)
    for bit in range(3):
        near_arrived(bit, other)

    def multiply(h):
        start = pl.multiple_of(h * chunk, chunk)
        return jnp.dot(
            all_ref[:, pl.ds(start, chunk)], cols_ref[pl.ds(start, chunk), :],
            preferred_element_type=jnp.float32,
        )

    hidden_ref[...] = multiply(high)

    def add(s, carry):
        for h, there in ((high - s, high - s >= 0), (high + s, high + s < highs)):
            @pl.when(there)
            def _(h=h):
                for l in range(SPLIT):
                    side(h, l, other).wait_recv()
                hidden_ref[...] += multiply(h)

        return carry

    lax.fori_loop(1, highs, add, 0)

    for bit in range(3):
        near(bit, 0).wait_send()
        near(bit, 1).wait_send()
    for p in range(PIECES):
        give(0, p).wait_send()
        give(1, p).wait_send()
        pass_on(p).wait_send()

    def sent(h, carry):
        for l in range(SPLIT):
            pl.when((h <= high) & (high < highs - 1))(lambda: line(True, h, l).wait_send())
            pl.when((h >= high) & (high > 0))(lambda: line(False, h, l).wait_send())
            pl.when(h != high)(lambda: side(h, l, part).wait_send())
        return carry

    lax.fori_loop(0, highs, sent, 0)


def pool(coarse, weight):
    rows, features = coarse.shape
    width = weight.shape[1] // SPLIT
    highs = lax.axis_size("tm") // SPLIT
    dma = pltpu.SemaphoreType.DMA
    vmem = pl.BlockSpec(memory_space=pltpu.VMEM)
    return pl.pallas_call(
        functools.partial(pool_kernel, highs),
        out_shape=jax.ShapeDtypeStruct((rows * SPLIT, width), jnp.float32),
        in_specs=[vmem, vmem],
        out_specs=vmem,
        scratch_shapes=[
            pltpu.VMEM((rows * SPLIT, features), jnp.bfloat16),
            pltpu.VMEM((features, width), jnp.bfloat16),
            [
                dma((3, 2)), dma((3, 2)), dma((2,)), dma((2, highs, SPLIT)), dma((highs, SPLIT)),
                dma((highs, SPLIT)), dma((highs, SPLIT)), dma((3, PIECES)), dma((3, PIECES)),
            ],
        ],
        compiler_params=pltpu.CompilerParams(collective_id=0, has_side_effects=True),
    )(coarse, weight)


def by_lanes(rows):
    return pl.BlockSpec((rows, LANES), lambda i: (0, i))


def tables(step_row, out_mix, skip_row, rows):
    modes = out_mix.shape[0]
    rates = step_row[None, :] * (jnp.arange(modes, dtype=jnp.float32) + 1.0)[:, None]
    in_scale = jnp.sqrt(-jnp.expm1(-2.0 * rates))
    out = out_mix * in_scale
    lags = jnp.arange(BLOCK, dtype=jnp.float32)
    kernel = jnp.sum(out[None] * jnp.exp(-lags[:, None, None] * rates[None]), axis=1)
    kernel = kernel.at[0].add(skip_row)
    powers = jnp.exp(-(lags + 1.0)[:, None] * step_row[None, :])
    return {
        "decay": jnp.exp(-rates),
        "step": jnp.exp(-rates * BLOCK),
        "whole": jnp.exp(-rates * rows),
        "out": out,
        "powers": powers,
        "kernel": kernel,
    }


def state_layer(hidden, gain, table, low_groups, high_groups):
    rows, chans = hidden.shape
    modes = table["decay"].shape[0]
    blocks = rows // BLOCK
    mean = jnp.mean(hidden, axis=-1)
    spread = jnp.sum(jnp.square(hidden - mean[:, None]), axis=-1)
    stats = lax.all_gather(jnp.stack([mean, spread]), "tm", axis_index_groups=low_groups)
    row_mean = jnp.mean(stats[:, 0], axis=0)
    row_var = (
        jnp.sum(stats[:, 1], axis=0) + chans * jnp.sum(jnp.square(stats[:, 0] - row_mean), axis=0)
    ) / (chans * SPLIT)
    normed = (hidden - row_mean[:, None]) * lax.rsqrt(row_var + 1e-05)[:, None] * gain[None, :]
    grid = (chans // LANES,)
    ends, last = pl.pallas_call(
        functools.partial(ends_kernel, modes),
        grid=grid,
        in_specs=[by_lanes(rows), by_lanes(modes), by_lanes(modes)],
        out_specs=[by_lanes(modes * blocks), by_lanes(modes)],
        out_shape=[
            jax.ShapeDtypeStruct((modes * blocks, chans), jnp.float32),
            jax.ShapeDtypeStruct((modes, chans), jnp.float32),
        ],
    )(normed, table["decay"], table["step"])
    every = lax.all_gather(last, "tm", axis_index_groups=high_groups)
    mine = lax.axis_index("tm") // SPLIT
    start = jnp.zeros_like(last)
    for p in range(len(high_groups[0]) - 1):
        start = jnp.where(p < mine, table["whole"] * start + every[p], start)
    return pl.pallas_call(
        functools.partial(respond_kernel, modes),
        grid=grid,
        in_specs=[
            by_lanes(rows), by_lanes(rows), by_lanes(modes * blocks), by_lanes(modes),
            by_lanes(modes), by_lanes(modes), by_lanes(BLOCK), by_lanes(BLOCK),
        ],
        out_specs=by_lanes(rows),
        out_shape=jax.ShapeDtypeStruct((rows, chans), jnp.float32),
        scratch_shapes=[pltpu.VMEM((modes * blocks, LANES), jnp.float32)],
    )(normed, hidden, ends, start, table["step"], table["out"], table["powers"], table["kernel"])


def local(signal, pool_weight, norm_gain, step_size, mode_out, skip_gain):
    fine_rows, channels = signal.shape
    count = lax.axis_size("tm")
    low = lax.axis_index("tm") % SPLIT
    low_groups = [[h * SPLIT + i for i in range(SPLIT)] for h in range(count // SPLIT)]
    high_groups = [[h * SPLIT + i for h in range(count // SPLIT)] for i in range(SPLIT)]
    coarse = signal.reshape(fine_rows // POOL, POOL * channels)
    hidden = pool(coarse, pool_weight)
    rows, chans = hidden.shape

    def own(array):
        return lax.dynamic_slice_in_dim(array, low * chans, chans, axis=array.ndim - 1)

    gain, step, mix, skip = own(norm_gain), own(step_size), own(mode_out), own(skip_gain)
    for l in range(norm_gain.shape[0]):
        table = tables(step[l], mix[l], skip[l], rows)
        hidden = state_layer(hidden, gain[l], table, low_groups, high_groups)
    return lax.all_to_all(
        hidden.astype(jnp.bfloat16), "tm", 0, 1, axis_index_groups=low_groups, tiled=True
    )


def solution(mesh):
    placed = (P(("parts", "tm"), None), P("tm", None), P(), P(), P(), P())
    return jax.shard_map(
        local, mesh=mesh, in_specs=placed, out_specs=P(("parts", "tm"), None), check_vma=False
    )
```

```python
import functools

import jax
import jax.numpy as jnp
from jax import lax
from jax.experimental import pallas as pl
from jax.experimental.pallas import tpu as pltpu
from jax.sharding import PartitionSpec as P

POOL = 4
SPLIT = 4
BLOCK = 16
LANES = 128
PIECES = 4


def block_ends(x_ref, decay_ref, ends_ref, modes, cols):
    rows = x_ref.shape[0]
    blocks = rows // BLOCK
    span = 8 * BLOCK

    def group(g, carry):
        base = pl.multiple_of(g * span, span)
        xs = [x_ref[pl.ds(base + j, 8, stride=BLOCK), cols] for j in range(BLOCK)]
        for n in range(modes):
            decay = jnp.broadcast_to(decay_ref[pl.ds(n, 1), cols], (8, LANES))
            end = xs[0]
            for j in range(1, BLOCK):
                end = end * decay + xs[j]
            ends_ref[pl.ds(pl.multiple_of(n * blocks + g * 8, 8), 8), cols] = end
        return carry

    lax.fori_loop(0, rows // span, group, 0)


def scan_blocks(ends_ref, step_ref, modes, cols, start, out_ref=None):
    blocks = ends_ref.shape[0] // modes
    groups = modes // 8
    steps = [step_ref[pl.ds(i * 8, 8), cols] for i in range(groups)]
    outs = [out_ref[pl.ds(i * 8, 8), cols] for i in range(groups)] if out_ref is not None else None
    states = list(start)
    for b in range(blocks):
        for i in range(groups):
            where = pl.ds(i * 8 * blocks + b, 8, stride=blocks)
            end = ends_ref[where, cols]
            if outs is not None:
                ends_ref[where, cols] = states[i] * outs[i]
            states[i] = states[i] * steps[i] + end
    return states


def respond(x_ref, hidden_ref, ends_ref, powers_ref, kernel_ref, result_ref, modes, cols):
    rows = x_ref.shape[0]
    blocks = rows // BLOCK
    span = 8 * BLOCK

    def group(g, carry):
        base = pl.multiple_of(g * span, span)
        coefs = [
            ends_ref[pl.ds(pl.multiple_of(n * blocks + g * 8, 8), 8), cols] for n in range(modes)
        ]
        xs = [x_ref[pl.ds(base + j, 8, stride=BLOCK), cols] for j in range(BLOCK)]
        for j in range(BLOCK):
            power = jnp.broadcast_to(powers_ref[pl.ds(j, 1), cols], (8, LANES))
            total = coefs[modes - 1]
            for n in range(modes - 2, -1, -1):
                total = total * power + coefs[n]
            total = total * power
            for i in range(j + 1):
                total = total + xs[i] * jnp.broadcast_to(
                    kernel_ref[pl.ds(j - i, 1), cols], (8, LANES)
                )
            where = pl.ds(base + j, 8, stride=BLOCK)
            gelu = 0.5 * total * (1.0 + lax.erf(total * 0.7071067811865476))
            result_ref[where, cols] = hidden_ref[where, cols] + gelu
        return carry

    lax.fori_loop(0, rows // span, group, 0)


MESH = pl.DeviceIdType.MESH


def pool_kernel(highs, coarse_ref, weight_ref, hidden_ref, all_ref, cols_ref, sems):
    part, place = lax.axis_index("parts"), lax.axis_index("tm")
    high, low = place // SPLIT, place % SPLIT
    depth, width = weight_ref.shape[0], cols_ref.shape[1]
    half = depth // 2
    rows = coarse_ref.shape[0]
    piece = rows // PIECES
    chunk = SPLIT * depth
    other = 1 - part
    (near_send, near_recv, own_sem, line_send, line_recv, side_send, side_recv,
     rows_send, rows_recv) = sems
    flip = lambda bit: low + bit - 2 * bit * ((low // bit) % 2)
    core, cross = flip(1), flip(2)
    diagonal = SPLIT - 1 - low
    at = lambda p, h, l: (p, h * SPLIT + l)

    barrier = pltpu.get_barrier_semaphore()

    def greet(device):
        pl.semaphore_signal(barrier, inc=1, device_id=device, device_id_type=MESH)

    for who in (core, cross, diagonal):
        greet(at(part, high, who))
    greet(at(other, high, low))
    pl.when(high > 0)(lambda: greet(at(part, high - 1, low)))
    pl.when(high < highs - 1)(lambda: greet(at(part, high + 1, low)))

    def spot(h, l, which):
        start = pl.multiple_of(h * chunk + l * depth + which * half, half)
        return cols_ref.at[pl.ds(start, half), :]

    def near(bit, which):
        to = (core, cross, diagonal)[bit]
        mine = weight_ref.at[
            pl.ds(pl.multiple_of(which * half, half), half),
            pl.ds(pl.multiple_of(to * width, width), width),
        ]
        return pltpu.make_async_remote_copy(
            mine, spot(high, low, which), near_send.at[bit, which], near_recv.at[bit, which],
            device_id=at(part, high, to), device_id_type=MESH,
        )

    def near_arrived(bit, which):
        who = (core, cross, diagonal)[bit]
        pltpu.make_async_remote_copy(
            spot(high, who, which), spot(high, who, which), near_send.at[bit, which],
            near_recv.at[bit, which], device_id=at(part, high, who), device_id_type=MESH,
        ).wait_recv()

    def line(up, h, l):
        to = jnp.clip(high + (1 if up else -1), 0, highs - 1)
        return pltpu.make_async_remote_copy(
            spot(h, l, part), spot(h, l, part), line_send.at[int(up), h, l], line_recv.at[h, l],
            device_id=at(part, to, low), device_id_type=MESH,
        )

    def side(h, l, which):
        return pltpu.make_async_remote_copy(
            spot(h, l, which), spot(h, l, which), side_send.at[h, l], side_recv.at[h, l],
            device_id=at(other, high, low), device_id_type=MESH,
        )

    def block(owner, p):
        start = pl.multiple_of(owner * rows + p * piece, piece)
        return all_ref.at[pl.ds(start, piece), :]

    def give(bit, p):
        to = core if bit == 0 else cross
        return pltpu.make_async_remote_copy(
            coarse_ref.at[pl.ds(p * piece, piece), :], block(low, p), rows_send.at[bit, p],
            rows_recv.at[bit, p], device_id=at(part, high, to), device_id_type=MESH,
        )

    def taken(bit, p):
        who = (core, cross, diagonal)[bit]
        pltpu.make_async_remote_copy(
            block(who, p), block(who, p), rows_send.at[bit, p], rows_recv.at[bit, p],
            device_id=at(part, high, core), device_id_type=MESH,
        ).wait_recv()

    def pass_on(p):
        return pltpu.make_async_remote_copy(
            block(cross, p), block(cross, p), rows_send.at[2, p], rows_recv.at[2, p],
            device_id=at(part, high, core), device_id_type=MESH,
        )

    own_weight = pltpu.make_async_copy(
        weight_ref.at[:, pl.ds(pl.multiple_of(low * width, width), width)],
        cols_ref.at[pl.ds(pl.multiple_of(high * chunk + low * depth, depth), depth), :],
        own_sem.at[0],
    )
    own_rows = pltpu.make_async_copy(
        coarse_ref, all_ref.at[pl.ds(pl.multiple_of(low * rows, rows), rows), :], own_sem.at[1]
    )
    own_weight.start()
    own_rows.start()
    ahead = jnp.minimum(high, 1) + jnp.minimum(highs - 1 - high, 1)
    pl.semaphore_wait(barrier, 4 + ahead)

    for bit in (1, 2, 0):
        near(bit, part).start()
    for p in range(PIECES):
        give(1, p).start()
    for p in range(PIECES):
        give(0, p).start()
    for bit in (1, 2, 0):
        near(bit, other).start()

    def both_ways(h, l):
        pl.when(high < highs - 1)(lambda: line(True, h, l).start())
        pl.when(high > 0)(lambda: line(False, h, l).start())

    own_weight.wait()
    both_ways(high, low)
    for bit, who in ((0, core), (1, cross), (2, diagonal)):
        near_arrived(bit, part)
        both_ways(high, who)

    def step(s, carry):
        for l in range(SPLIT):
            @pl.when(high - s >= 0)
            def _():
                h = high - s
                line(True, h, l).wait_recv()
                pl.when(high < highs - 1)(lambda: line(True, h, l).start())
                side(h, l, part).start()

            @pl.when(high + s < highs)
            def _():
                h = high + s
                line(False, h, l).wait_recv()
                pl.when(high > 0)(lambda: line(False, h, l).start())
                side(h, l, part).start()

        @pl.when(s < PIECES)
        def _():
            taken(1, s - 1)
            pass_on(s - 1).start()

        return carry

    lax.fori_loop(1, highs, step, 0)
    for p in range(min(PIECES - 1, highs - 1), PIECES):
        taken(1, p)
        pass_on(p).start()
    own_rows.wait()
    for p in range(PIECES):
        taken(0, p)
        taken(2, p)
    for bit in range(3):
        near_arrived(bit, other)

    def multiply(h):
        start = pl.multiple_of(h * chunk, chunk)
        return jnp.dot(
            all_ref[:, pl.ds(start, chunk)], cols_ref[pl.ds(start, chunk), :],
            preferred_element_type=jnp.float32,
        )

    def keep(value, first):
        for g in range(width // LANES):
            piece_of = value[:, g * LANES : (g + 1) * LANES]
            hidden_ref[g] = piece_of if first else hidden_ref[g] + piece_of

    keep(multiply(high), True)

    def add(s, carry):
        for h, there in ((high - s, high - s >= 0), (high + s, high + s < highs)):
            @pl.when(there)
            def _(h=h):
                for l in range(SPLIT):
                    side(h, l, other).wait_recv()
                keep(multiply(h), False)

        return carry

    lax.fori_loop(1, highs, add, 0)

    for bit in range(3):
        near(bit, 0).wait_send()
        near(bit, 1).wait_send()
    for p in range(PIECES):
        give(0, p).wait_send()
        give(1, p).wait_send()
        pass_on(p).wait_send()

    def sent(h, carry):
        for l in range(SPLIT):
            pl.when((h <= high) & (high < highs - 1))(lambda: line(True, h, l).wait_send())
            pl.when((h >= high) & (high > 0))(lambda: line(False, h, l).wait_send())
            pl.when(h != high)(lambda: side(h, l, part).wait_send())
        return carry

    lax.fori_loop(0, highs, sent, 0)


def pool(coarse, weight):
    rows, features = coarse.shape
    width = weight.shape[1] // SPLIT
    highs = lax.axis_size("tm") // SPLIT
    dma = pltpu.SemaphoreType.DMA
    vmem = pl.BlockSpec(memory_space=pltpu.VMEM)
    return pl.pallas_call(
        functools.partial(pool_kernel, highs),
        out_shape=jax.ShapeDtypeStruct((width // LANES, rows * SPLIT, LANES), jnp.float32),
        in_specs=[vmem, vmem],
        out_specs=vmem,
        scratch_shapes=[
            pltpu.VMEM((rows * SPLIT, features), jnp.bfloat16),
            pltpu.VMEM((features, width), jnp.bfloat16),
            [
                dma((3, 2)), dma((3, 2)), dma((2,)), dma((2, highs, SPLIT)), dma((highs, SPLIT)),
                dma((highs, SPLIT)), dma((highs, SPLIT)), dma((3, PIECES)), dma((3, PIECES)),
            ],
        ],
        compiler_params=pltpu.CompilerParams(collective_id=0, has_side_effects=True),
    )(coarse, weight)


def tables(step_row, out_mix, skip_row, rows):
    modes = out_mix.shape[0]
    rates = step_row[None, :] * (jnp.arange(modes, dtype=jnp.float32) + 1.0)[:, None]
    in_scale = jnp.sqrt(-jnp.expm1(-2.0 * rates))
    out = out_mix * in_scale
    lags = jnp.arange(BLOCK, dtype=jnp.float32)
    kernel = jnp.sum(out[None] * jnp.exp(-lags[:, None, None] * rates[None]), axis=1)
    kernel = kernel.at[0].add(skip_row)
    powers = jnp.exp(-(lags + 1.0)[:, None] * step_row[None, :])
    return jnp.concatenate(
        [jnp.exp(-rates), jnp.exp(-rates * BLOCK), jnp.exp(-rates * rows), out]
        + [jnp.pad(extra, ((0, modes - BLOCK), (0, 0))) for extra in (powers, kernel)]
    )


def layers_kernel(
    highs, modes, hidden_in_ref, gain_ref, table_ref, out_ref, hidden_ref, x_ref, ends_ref,
    stats_ref, last_ref, states_ref, rounded_ref, sems
):
    stats_send, stats_recv, state_send, state_recv, out_send, out_recv = sems
    part, place = lax.axis_index("parts"), lax.axis_index("tm")
    high, low = place // SPLIT, place % SPLIT
    groups, rows, _ = hidden_in_ref.shape
    chans = groups * LANES
    layers = gain_ref.shape[0]
    flip = lambda bit: low + bit - 2 * bit * ((low // bit) % 2)
    near = (flip(1), flip(2), SPLIT - 1 - low)
    at = lambda h, l: (part, h * SPLIT + l)
    own_rows = rows // SPLIT
    exact = lax.Precision.HIGHEST

    barrier = pltpu.get_barrier_semaphore()

    def greet(device):
        pl.semaphore_signal(barrier, inc=1, device_id=device, device_id_type=MESH)

    for who in near:
        greet(at(high, who))

    def greet_high(h, carry):
        pl.when(h != high)(lambda: greet(at(h, low)))
        return carry

    lax.fori_loop(0, highs, greet_high, 0)

    def stats_copy(l, bit, owner):
        return pltpu.make_async_remote_copy(
            stats_ref.at[l, owner], stats_ref.at[l, owner], stats_send.at[l, bit],
            stats_recv.at[l, bit], device_id=at(high, near[bit]), device_id_type=MESH,
        )

    def state_copy(l, g, source, target):
        return pltpu.make_async_remote_copy(
            last_ref.at[l, g], states_ref.at[l, source, g], state_send.at[l, target, g],
            state_recv.at[l, source, g], device_id=at(target, low), device_id_type=MESH,
        )

    def out_cols(owner, g):
        return pl.ds(pl.multiple_of(owner * chans + g * LANES, LANES), LANES)

    def out_copy(g, bit, owner):
        start = pl.multiple_of(near[bit] * own_rows, own_rows)
        return pltpu.make_async_remote_copy(
            rounded_ref.at[g, pl.ds(start, own_rows), :], out_ref.at[:, out_cols(owner, g)],
            out_send.at[g, bit], out_recv.at[g, bit],
            device_id=at(high, near[bit]), device_id_type=MESH,
        )

    for l in range(layers):
        source_ref = hidden_in_ref if l == 0 else hidden_ref
        total = source_ref[0]
        for g in range(1, groups):
            total = total + source_ref[g]
        mean = jnp.sum(total, axis=-1, keepdims=True) / chans
        square = jnp.square(source_ref[0] - mean)
        for g in range(1, groups):
            square = square + jnp.square(source_ref[g] - mean)
        ones = jnp.ones((8, LANES), jnp.float32)
        across = lambda v: lax.dot_general(
            ones, v, (((1,), (1,)), ((), ())), precision=exact, preferred_element_type=jnp.float32
        )
        line = lax.broadcasted_iota(jnp.int32, (8, rows), 0)
        stats_ref[l, low] = jnp.where(line == 0, across(total) / chans, across(square))
        if l == 0:
            pl.semaphore_wait(barrier, 3 + highs - 1)
        for bit in (1, 2, 0):
            stats_copy(l, bit, low).start()
        for bit in range(3):
            stats_copy(l, bit, near[bit]).wait_recv()
        every = [stats_ref[l, i] for i in range(SPLIT)]
        means = [e[0:1] for e in every]
        row_mean = (means[0] + means[1] + means[2] + means[3]) / SPLIT
        row_var = sum(e[1:2] + chans * jnp.square(e[0:1] - row_mean) for e in every)
        row_scale = lax.rsqrt(row_var / (chans * SPLIT) + 1e-05)
        both = jnp.where(line == 0, row_mean, row_scale)
        both = jnp.transpose(both)
        row_mean, row_scale = both[:, 0:1], both[:, 1:2]
        for g in range(groups):
            gain = gain_ref[pl.ds(l, 1), pl.ds(g * LANES, LANES)]
            x_ref[g] = (source_ref[g] - row_mean) * row_scale * gain

        def table(index, g, size):
            return table_ref.at[l, pl.ds(index * modes, size), pl.ds(pl.multiple_of(g * LANES, LANES), LANES)]

        cols = slice(None)
        eights = modes // 8

        def send(g):
            def one(h, carry):
                pl.when(h > high)(lambda: state_copy(l, g, high, h).start())
                return carry

            lax.fori_loop(1, highs, one, 0)

        def ends(g, carry):
            block_ends(x_ref.at[g], table(0, g, modes), ends_ref.at[g], modes, cols)
            zero = [jnp.zeros((8, LANES), jnp.float32)] * eights
            last = scan_blocks(ends_ref.at[g], table(1, g, modes), modes, cols, zero)
            for i in range(eights):
                last_ref[l, g, pl.ds(i * 8, 8), :] = last[i]
            send(g)
            return carry

        lax.fori_loop(0, groups, ends, 0)

        def finish(g, carry):
            whole = table(2, g, modes)

            def join(h, start):
                @pl.when(h < high)
                def _():
                    state_copy(l, g, h, high).wait_recv()
                    states_ref[l, high, g] = whole[...] * states_ref[l, high, g] + states_ref[l, h, g]
                return start

            states_ref[l, high, g] = jnp.zeros((modes, LANES), jnp.float32)
            lax.fori_loop(0, highs - 1, join, 0)
            start = [states_ref[l, high, g, pl.ds(i * 8, 8), :] for i in range(eights)]
            scan_blocks(
                ends_ref.at[g], table(1, g, modes), modes, cols, start, table(3, g, modes)
            )
            respond(
                x_ref.at[g], source_ref.at[g], ends_ref.at[g], table(4, g, BLOCK),
                table(5, g, BLOCK), hidden_ref.at[g], modes, cols,
            )
            if l == layers - 1:
                rounded_ref[g] = hidden_ref[g].astype(jnp.bfloat16)
                for bit in (1, 2, 0):
                    out_copy(g, bit, low).start()
                out_ref[:, out_cols(low, g)] = rounded_ref[
                    g, pl.ds(pl.multiple_of(low * own_rows, own_rows), own_rows), :
                ]
            return carry

        lax.fori_loop(0, groups, finish, 0)

    def drain(g, carry):
        for bit in range(3):
            out_copy(g, bit, near[bit]).wait_recv()
            out_copy(g, bit, low).wait_send()

        def one(h, carry):
            @pl.when(h > high)
            def _():
                for l in range(layers):
                    state_copy(l, g, high, h).wait_send()
            return carry

        return lax.fori_loop(1, highs, one, carry)

    lax.fori_loop(0, groups, drain, 0)
    for l in range(layers):
        for bit in range(3):
            stats_copy(l, bit, low).wait_send()


def run_layers(hidden, gain, table, modes):
    groups, rows, _ = hidden.shape
    layers = gain.shape[0]
    highs = lax.axis_size("tm") // SPLIT
    dma = pltpu.SemaphoreType.DMA
    vmem = pl.BlockSpec(memory_space=pltpu.VMEM)
    f32 = jnp.float32
    return pl.pallas_call(
        functools.partial(layers_kernel, highs, modes),
        out_shape=jax.ShapeDtypeStruct((rows // SPLIT, groups * LANES * SPLIT), jnp.bfloat16),
        in_specs=[vmem] * 3,
        out_specs=vmem,
        scratch_shapes=[
            pltpu.VMEM((groups, rows, LANES), f32),
            pltpu.VMEM((groups, rows, LANES), f32),
            pltpu.VMEM((groups, modes * (rows // BLOCK), LANES), f32),
            pltpu.VMEM((layers, SPLIT, 8, rows), f32),
            pltpu.VMEM((layers, groups, modes, LANES), f32),
            pltpu.VMEM((layers, highs, groups, modes, LANES), f32),
            pltpu.VMEM((groups, rows, LANES), jnp.bfloat16),
            [
                dma((layers, 3)), dma((layers, 3)), dma((layers, highs, groups)),
                dma((layers, highs, groups)), dma((groups, 3)), dma((groups, 3)),
            ],
        ],
        compiler_params=pltpu.CompilerParams(collective_id=1, has_side_effects=True),
    )(hidden, gain, table)


def local(signal, pool_weight, norm_gain, step_size, mode_out, skip_gain):
    fine_rows, channels = signal.shape
    low = lax.axis_index("tm") % SPLIT
    coarse = signal.reshape(fine_rows // POOL, POOL * channels)
    chans = pool_weight.shape[1] // SPLIT
    rows = SPLIT * coarse.shape[0]
    modes = mode_out.shape[1]

    def own(array):
        return lax.dynamic_slice_in_dim(array, low * chans, chans, axis=array.ndim - 1)

    gain, step, mix, skip = own(norm_gain), own(step_size), own(mode_out), own(skip_gain)
    table = jax.vmap(functools.partial(tables, rows=rows))(step, mix, skip)
    hidden = pool(coarse, pool_weight)
    return run_layers(hidden, gain, table, modes)


def solution(mesh):
    placed = (P(("parts", "tm"), None), P("tm", None), P(), P(), P(), P())
    return jax.shard_map(
        local, mesh=mesh, in_specs=placed, out_specs=P(("parts", "tm"), None), check_vma=False
    )
```

```python
import functools

import jax
import jax.numpy as jnp
from jax import lax
from jax.experimental import pallas as pl
from jax.experimental.pallas import tpu as pltpu
from jax.sharding import PartitionSpec as P

POOL = 4
SPLIT = 4
BLOCK = 16
LANES = 128
PIECES = 4
PAD = 8


def block_ends(x_ref, decay_ref, ends_ref, modes, cols):
    rows = x_ref.shape[0]
    blocks = rows // BLOCK
    span = 8 * BLOCK
    pitch = ends_ref.shape[0] // blocks

    def group(g, carry):
        base = pl.multiple_of(g * span, span)
        xs = [x_ref[pl.ds(base + j, 8, stride=BLOCK), cols] for j in range(BLOCK)]
        for n in range(modes):
            decay = jnp.broadcast_to(decay_ref[pl.ds(n, 1), cols], (8, LANES))
            end = xs[0]
            for j in range(1, BLOCK):
                end = end * decay + xs[j]
            ends_ref[pl.ds(g * 8 * pitch + n, 8, stride=pitch), cols] = end
        return carry

    lax.fori_loop(0, rows // span, group, 0)


def scan_blocks(blocks, ends_ref, step_ref, modes, cols, start, out_ref=None):
    pitch = ends_ref.shape[0] // blocks
    groups = modes // 8
    steps = [step_ref[pl.ds(i * 8, 8), cols] for i in range(groups)]
    outs = [out_ref[pl.ds(i * 8, 8), cols] for i in range(groups)] if out_ref is not None else None
    states = list(start)
    for b in range(blocks):
        for i in range(groups):
            where = pl.ds(b * pitch + i * 8, 8)
            end = ends_ref[where, cols]
            if outs is not None:
                ends_ref[where, cols] = states[i] * outs[i]
            states[i] = states[i] * steps[i] + end
    return states


def respond(x_ref, hidden_ref, ends_ref, powers_ref, kernel_ref, result_ref, modes, cols):
    rows = x_ref.shape[0]
    blocks = rows // BLOCK
    span = 8 * BLOCK
    pitch = ends_ref.shape[0] // blocks

    def group(g, carry):
        base = pl.multiple_of(g * span, span)
        coefs = [ends_ref[pl.ds(g * 8 * pitch + n, 8, stride=pitch), cols] for n in range(modes)]
        xs = [x_ref[pl.ds(base + j, 8, stride=BLOCK), cols] for j in range(BLOCK)]
        for j in range(BLOCK):
            power = jnp.broadcast_to(powers_ref[pl.ds(j, 1), cols], (8, LANES))
            total = coefs[modes - 1]
            for n in range(modes - 2, -1, -1):
                total = total * power + coefs[n]
            total = total * power
            for i in range(j + 1):
                total = total + xs[i] * jnp.broadcast_to(
                    kernel_ref[pl.ds(j - i, 1), cols], (8, LANES)
                )
            where = pl.ds(base + j, 8, stride=BLOCK)
            gelu = 0.5 * total * (1.0 + lax.erf(total * 0.7071067811865476))
            result_ref[where, cols] = hidden_ref[where, cols] + gelu
        return carry

    lax.fori_loop(0, rows // span, group, 0)


MESH = pl.DeviceIdType.MESH


def pool_kernel(highs, coarse_ref, weight_ref, hidden_ref, all_ref, cols_ref, sems):
    part, place = lax.axis_index("parts"), lax.axis_index("tm")
    high, low = place // SPLIT, place % SPLIT
    depth, width = weight_ref.shape[0], cols_ref.shape[1]
    half = depth // 2
    rows = coarse_ref.shape[0]
    piece = rows // PIECES
    chunk = SPLIT * depth
    other = 1 - part
    (near_send, near_recv, own_sem, line_send, line_recv, side_send, side_recv,
     rows_send, rows_recv) = sems
    flip = lambda bit: low + bit - 2 * bit * ((low // bit) % 2)
    core, cross = flip(1), flip(2)
    diagonal = SPLIT - 1 - low
    at = lambda p, h, l: (p, h * SPLIT + l)

    barrier = pltpu.get_barrier_semaphore()

    def greet(device):
        pl.semaphore_signal(barrier, inc=1, device_id=device, device_id_type=MESH)

    for who in (core, cross, diagonal):
        greet(at(part, high, who))
    greet(at(other, high, low))
    pl.when(high > 0)(lambda: greet(at(part, high - 1, low)))
    pl.when(high < highs - 1)(lambda: greet(at(part, high + 1, low)))

    def spot(h, l, which):
        start = pl.multiple_of(h * chunk + l * depth + which * half, half)
        return cols_ref.at[pl.ds(start, half), :]

    def near(bit, which):
        to = (core, cross, diagonal)[bit]
        mine = weight_ref.at[
            pl.ds(pl.multiple_of(which * half, half), half),
            pl.ds(pl.multiple_of(to * width, width), width),
        ]
        return pltpu.make_async_remote_copy(
            mine, spot(high, low, which), near_send.at[bit, which], near_recv.at[bit, which],
            device_id=at(part, high, to), device_id_type=MESH,
        )

    def near_arrived(bit, which):
        who = (core, cross, diagonal)[bit]
        pltpu.make_async_remote_copy(
            spot(high, who, which), spot(high, who, which), near_send.at[bit, which],
            near_recv.at[bit, which], device_id=at(part, high, who), device_id_type=MESH,
        ).wait_recv()

    def line(up, h, l):
        to = jnp.clip(high + (1 if up else -1), 0, highs - 1)
        return pltpu.make_async_remote_copy(
            spot(h, l, part), spot(h, l, part), line_send.at[int(up), h, l], line_recv.at[h, l],
            device_id=at(part, to, low), device_id_type=MESH,
        )

    def side(h, l, which):
        return pltpu.make_async_remote_copy(
            spot(h, l, which), spot(h, l, which), side_send.at[h, l], side_recv.at[h, l],
            device_id=at(other, high, low), device_id_type=MESH,
        )

    def block(owner, p):
        start = pl.multiple_of(owner * rows + p * piece, piece)
        return all_ref.at[pl.ds(start, piece), :]

    def give(bit, p):
        to = core if bit == 0 else cross
        return pltpu.make_async_remote_copy(
            coarse_ref.at[pl.ds(p * piece, piece), :], block(low, p), rows_send.at[bit, p],
            rows_recv.at[bit, p], device_id=at(part, high, to), device_id_type=MESH,
        )

    def taken(bit, p):
        who = (core, cross, diagonal)[bit]
        pltpu.make_async_remote_copy(
            block(who, p), block(who, p), rows_send.at[bit, p], rows_recv.at[bit, p],
            device_id=at(part, high, core), device_id_type=MESH,
        ).wait_recv()

    def pass_on(p):
        return pltpu.make_async_remote_copy(
            block(cross, p), block(cross, p), rows_send.at[2, p], rows_recv.at[2, p],
            device_id=at(part, high, core), device_id_type=MESH,
        )

    own_weight = pltpu.make_async_copy(
        weight_ref.at[:, pl.ds(pl.multiple_of(low * width, width), width)],
        cols_ref.at[pl.ds(pl.multiple_of(high * chunk + low * depth, depth), depth), :],
        own_sem.at[0],
    )
    own_rows = pltpu.make_async_copy(
        coarse_ref, all_ref.at[pl.ds(pl.multiple_of(low * rows, rows), rows), :], own_sem.at[1]
    )
    own_weight.start()
    own_rows.start()
    ahead = jnp.minimum(high, 1) + jnp.minimum(highs - 1 - high, 1)
    pl.semaphore_wait(barrier, 4 + ahead)

    for bit in (1, 2, 0):
        near(bit, part).start()
    for p in range(PIECES):
        give(1, p).start()
    for p in range(PIECES):
        give(0, p).start()
    for bit in (1, 2, 0):
        near(bit, other).start()

    def both_ways(h, l):
        pl.when(high < highs - 1)(lambda: line(True, h, l).start())
        pl.when(high > 0)(lambda: line(False, h, l).start())

    own_weight.wait()
    both_ways(high, low)
    for bit, who in ((0, core), (1, cross), (2, diagonal)):
        near_arrived(bit, part)
        both_ways(high, who)

    def relay(s, l):
        @pl.when(high - s >= 0)
        def _():
            h = high - s
            line(True, h, l).wait_recv()
            pl.when(high < highs - 1)(lambda: line(True, h, l).start())
            side(h, l, part).start()

        @pl.when(high + s < highs)
        def _():
            h = high + s
            line(False, h, l).wait_recv()
            pl.when(high > 0)(lambda: line(False, h, l).start())
            side(h, l, part).start()

    def step(s, carry):
        for l in range(SPLIT):
            relay(s, l)

        @pl.when(s < PIECES)
        def _():
            taken(1, s - 1)
            pass_on(s - 1).start()

        return carry

    last = highs - 1
    lax.fori_loop(1, last, step, 0)
    for l in range(SPLIT - 1):
        relay(last, l)
    for p in range(min(PIECES - 1, last - 1), PIECES):
        taken(1, p)
        pass_on(p).start()
    own_rows.wait()
    for p in range(PIECES):
        taken(0, p)
        taken(2, p)
    for bit in range(3):
        near_arrived(bit, other)

    def multiply(h):
        start = pl.multiple_of(h * chunk, chunk)
        return jnp.dot(
            all_ref[:, pl.ds(start, chunk)], cols_ref[pl.ds(start, chunk), :],
            preferred_element_type=jnp.float32,
        )

    def keep(value, first):
        for g in range(width // LANES):
            piece_of = value[:, g * LANES : (g + 1) * LANES]
            hidden_ref[g] = piece_of if first else hidden_ref[g] + piece_of

    keep(multiply(high), True)

    def add(s, carry):
        for h, there in ((high - s, high - s >= 0), (high + s, high + s < highs)):
            @pl.when(there)
            def _(h=h):
                for l in range(SPLIT):
                    side(h, l, other).wait_recv()
                keep(multiply(h), False)

        return carry

    lax.fori_loop(1, last, add, 0)
    relay(last, SPLIT - 1)
    add(last, 0)

    for bit in range(3):
        near(bit, 0).wait_send()
        near(bit, 1).wait_send()
    for p in range(PIECES):
        give(0, p).wait_send()
        give(1, p).wait_send()
        pass_on(p).wait_send()

    def sent(h, carry):
        for l in range(SPLIT):
            pl.when((h <= high) & (high < highs - 1))(lambda: line(True, h, l).wait_send())
            pl.when((h >= high) & (high > 0))(lambda: line(False, h, l).wait_send())
            pl.when(h != high)(lambda: side(h, l, part).wait_send())
        return carry

    lax.fori_loop(0, highs, sent, 0)


def pool(coarse, weight):
    rows, features = coarse.shape
    width = weight.shape[1] // SPLIT
    highs = lax.axis_size("tm") // SPLIT
    dma = pltpu.SemaphoreType.DMA
    vmem = pl.BlockSpec(memory_space=pltpu.VMEM)
    return pl.pallas_call(
        functools.partial(pool_kernel, highs),
        out_shape=jax.ShapeDtypeStruct((width // LANES, rows * SPLIT, LANES), jnp.float32),
        in_specs=[vmem, vmem],
        out_specs=vmem,
        scratch_shapes=[
            pltpu.VMEM((rows * SPLIT, features), jnp.bfloat16),
            pltpu.VMEM((features, width), jnp.bfloat16),
            [
                dma((3, 2)), dma((3, 2)), dma((2,)), dma((2, highs, SPLIT)), dma((highs, SPLIT)),
                dma((highs, SPLIT)), dma((highs, SPLIT)), dma((3, PIECES)), dma((3, PIECES)),
            ],
        ],
        compiler_params=pltpu.CompilerParams(collective_id=0, has_side_effects=True),
    )(coarse, weight)


def tables(step_row, out_mix, skip_row, rows):
    modes = out_mix.shape[0]
    rates = step_row[None, :] * (jnp.arange(modes, dtype=jnp.float32) + 1.0)[:, None]
    in_scale = jnp.sqrt(-jnp.expm1(-2.0 * rates))
    out = out_mix * in_scale
    lags = jnp.arange(BLOCK, dtype=jnp.float32)
    kernel = jnp.sum(out[None] * jnp.exp(-lags[:, None, None] * rates[None]), axis=1)
    kernel = kernel.at[0].add(skip_row)
    powers = jnp.exp(-(lags + 1.0)[:, None] * step_row[None, :])
    return jnp.concatenate(
        [jnp.exp(-rates), jnp.exp(-rates * BLOCK), jnp.exp(-rates * rows), out]
        + [jnp.pad(extra, ((0, modes - BLOCK), (0, 0))) for extra in (powers, kernel)]
    )


def layers_kernel(
    highs, modes, hidden_in_ref, gain_ref, table_ref, out_ref, hidden_ref, x_ref, ends_ref,
    stats_ref, last_ref, states_ref, rounded_ref, sems
):
    stats_send, stats_recv, state_send, state_recv, out_send, out_recv = sems
    part, place = lax.axis_index("parts"), lax.axis_index("tm")
    high, low = place // SPLIT, place % SPLIT
    groups, rows, _ = hidden_in_ref.shape
    chans = groups * LANES
    layers = gain_ref.shape[0]
    flip = lambda bit: low + bit - 2 * bit * ((low // bit) % 2)
    near = (flip(1), flip(2), SPLIT - 1 - low)
    at = lambda h, l: (part, h * SPLIT + l)
    own_rows = rows // SPLIT
    blocks = rows // BLOCK
    exact = lax.Precision.HIGHEST

    barrier = pltpu.get_barrier_semaphore()

    def greet(device):
        pl.semaphore_signal(barrier, inc=1, device_id=device, device_id_type=MESH)

    for who in near:
        greet(at(high, who))

    def greet_high(h, carry):
        pl.when(h != high)(lambda: greet(at(h, low)))
        return carry

    lax.fori_loop(0, highs, greet_high, 0)

    def stats_copy(l, bit, owner):
        return pltpu.make_async_remote_copy(
            stats_ref.at[l, owner], stats_ref.at[l, owner], stats_send.at[l, bit],
            stats_recv.at[l, bit], device_id=at(high, near[bit]), device_id_type=MESH,
        )

    def state_copy(l, g, source, target):
        return pltpu.make_async_remote_copy(
            last_ref.at[l, g], states_ref.at[l, source, g], state_send.at[l, target, g],
            state_recv.at[l, source, g], device_id=at(target, low), device_id_type=MESH,
        )

    def out_cols(owner, g):
        return pl.ds(pl.multiple_of(owner * chans + g * LANES, LANES), LANES)

    def out_copy(g, bit, owner):
        start = pl.multiple_of(near[bit] * own_rows, own_rows)
        return pltpu.make_async_remote_copy(
            rounded_ref.at[g, pl.ds(start, own_rows), :], out_ref.at[:, out_cols(owner, g)],
            out_send.at[g, bit], out_recv.at[g, bit],
            device_id=at(high, near[bit]), device_id_type=MESH,
        )

    for l in range(layers):
        source_ref = hidden_in_ref if l == 0 else hidden_ref
        total = source_ref[0]
        for g in range(1, groups):
            total = total + source_ref[g]
        mean = jnp.sum(total, axis=-1, keepdims=True) / chans
        square = jnp.square(source_ref[0] - mean)
        for g in range(1, groups):
            square = square + jnp.square(source_ref[g] - mean)
        ones = jnp.ones((8, LANES), jnp.float32)
        across = lambda v: lax.dot_general(
            ones, v, (((1,), (1,)), ((), ())), precision=exact, preferred_element_type=jnp.float32
        )
        line = lax.broadcasted_iota(jnp.int32, (8, rows), 0)
        stats_ref[l, low] = jnp.where(line == 0, across(total) / chans, across(square))
        if l == 0:
            pl.semaphore_wait(barrier, 3 + highs - 1)
        for bit in (1, 2, 0):
            stats_copy(l, bit, low).start()
        for bit in range(3):
            stats_copy(l, bit, near[bit]).wait_recv()
        every = [stats_ref[l, i] for i in range(SPLIT)]
        means = [e[0:1] for e in every]
        row_mean = (means[0] + means[1] + means[2] + means[3]) / SPLIT
        row_var = sum(e[1:2] + chans * jnp.square(e[0:1] - row_mean) for e in every)
        row_scale = lax.rsqrt(row_var / (chans * SPLIT) + 1e-05)
        both = jnp.where(line == 0, row_mean, row_scale)
        both = jnp.transpose(both)
        row_mean, row_scale = both[:, 0:1], both[:, 1:2]
        for g in range(groups):
            gain = gain_ref[pl.ds(l, 1), pl.ds(g * LANES, LANES)]
            x_ref[g] = (source_ref[g] - row_mean) * row_scale * gain

        def table(index, g, size):
            return table_ref.at[l, pl.ds(index * modes, size), pl.ds(pl.multiple_of(g * LANES, LANES), LANES)]

        cols = slice(None)
        eights = modes // 8

        def send(g):
            def one(h, carry):
                pl.when(h > high)(lambda: state_copy(l, g, high, h).start())
                return carry

            lax.fori_loop(1, highs, one, 0)

        def ends(g, carry):
            block_ends(x_ref.at[g], table(0, g, modes), ends_ref.at[g], modes, cols)
            zero = [jnp.zeros((8, LANES), jnp.float32)] * eights
            last = scan_blocks(blocks, ends_ref.at[g], table(1, g, modes), modes, cols, zero)
            for i in range(eights):
                last_ref[l, g, pl.ds(i * 8, 8), :] = last[i]
            send(g)
            return carry

        lax.fori_loop(0, groups, ends, 0)

        def finish(g, carry):
            whole = table(2, g, modes)

            def join(h, start):
                @pl.when(h < high)
                def _():
                    state_copy(l, g, h, high).wait_recv()
                    states_ref[l, high, g] = whole[...] * states_ref[l, high, g] + states_ref[l, h, g]
                return start

            states_ref[l, high, g] = jnp.zeros((modes, LANES), jnp.float32)
            lax.fori_loop(0, highs - 1, join, 0)
            start = [states_ref[l, high, g, pl.ds(i * 8, 8), :] for i in range(eights)]
            scan_blocks(
                blocks, ends_ref.at[g], table(1, g, modes), modes, cols, start, table(3, g, modes)
            )
            respond(
                x_ref.at[g], source_ref.at[g], ends_ref.at[g], table(4, g, BLOCK),
                table(5, g, BLOCK), hidden_ref.at[g], modes, cols,
            )
            if l == layers - 1:
                rounded_ref[g] = hidden_ref[g].astype(jnp.bfloat16)
                for bit in (1, 2, 0):
                    out_copy(g, bit, low).start()
                out_ref[:, out_cols(low, g)] = rounded_ref[
                    g, pl.ds(pl.multiple_of(low * own_rows, own_rows), own_rows), :
                ]
            return carry

        lax.fori_loop(0, groups, finish, 0)

    def drain(g, carry):
        for bit in range(3):
            out_copy(g, bit, near[bit]).wait_recv()
            out_copy(g, bit, low).wait_send()

        def one(h, carry):
            @pl.when(h > high)
            def _():
                for l in range(layers):
                    state_copy(l, g, high, h).wait_send()
            return carry

        return lax.fori_loop(1, highs, one, carry)

    lax.fori_loop(0, groups, drain, 0)
    for l in range(layers):
        for bit in range(3):
            stats_copy(l, bit, low).wait_send()


def run_layers(hidden, gain, table, modes):
    groups, rows, _ = hidden.shape
    layers = gain.shape[0]
    highs = lax.axis_size("tm") // SPLIT
    dma = pltpu.SemaphoreType.DMA
    vmem = pl.BlockSpec(memory_space=pltpu.VMEM)
    f32 = jnp.float32
    return pl.pallas_call(
        functools.partial(layers_kernel, highs, modes),
        out_shape=jax.ShapeDtypeStruct((rows // SPLIT, groups * LANES * SPLIT), jnp.bfloat16),
        in_specs=[vmem] * 3,
        out_specs=vmem,
        scratch_shapes=[
            pltpu.VMEM((groups, rows, LANES), f32),
            pltpu.VMEM((groups, rows, LANES), f32),
            pltpu.VMEM((groups, (modes + PAD) * (rows // BLOCK), LANES), f32),
            pltpu.VMEM((layers, SPLIT, 8, rows), f32),
            pltpu.VMEM((layers, groups, modes, LANES), f32),
            pltpu.VMEM((layers, highs, groups, modes, LANES), f32),
            pltpu.VMEM((groups, rows, LANES), jnp.bfloat16),
            [
                dma((layers, 3)), dma((layers, 3)), dma((layers, highs, groups)),
                dma((layers, highs, groups)), dma((groups, 3)), dma((groups, 3)),
            ],
        ],
        compiler_params=pltpu.CompilerParams(collective_id=1, has_side_effects=True),
    )(hidden, gain, table)


def local(signal, pool_weight, norm_gain, step_size, mode_out, skip_gain):
    fine_rows, channels = signal.shape
    low = lax.axis_index("tm") % SPLIT
    coarse = signal.reshape(fine_rows // POOL, POOL * channels)
    chans = pool_weight.shape[1] // SPLIT
    rows = SPLIT * coarse.shape[0]
    modes = mode_out.shape[1]

    def own(array):
        return lax.dynamic_slice_in_dim(array, low * chans, chans, axis=array.ndim - 1)

    gain, step, mix, skip = own(norm_gain), own(step_size), own(mode_out), own(skip_gain)
    table = jax.vmap(functools.partial(tables, rows=rows))(step, mix, skip)
    hidden = pool(coarse, pool_weight)
    return run_layers(hidden, gain, table, modes)


def solution(mesh):
    placed = (P(("parts", "tm"), None), P("tm", None), P(), P(), P(), P())
    return jax.shard_map(
        local, mesh=mesh, in_specs=placed, out_specs=P(("parts", "tm"), None), check_vma=False
    )
```

```python
import functools

import jax
import jax.numpy as jnp
from jax import lax
from jax.experimental import pallas as pl
from jax.experimental.pallas import tpu as pltpu
from jax.sharding import PartitionSpec as P

POOL = 4
SPLIT = 4
BLOCK = 16
LANES = 128
PIECES = 4
PAD = 1


def block_ends(x_ref, decay_ref, ends_ref, modes, cols):
    rows = x_ref.shape[0]
    blocks = rows // BLOCK
    span = 8 * BLOCK
    pitch = ends_ref.shape[0] // blocks

    def group(g, carry):
        base = pl.multiple_of(g * span, span)
        xs = [x_ref[pl.ds(base + j, 8, stride=BLOCK), cols] for j in range(BLOCK)]
        for n in range(modes):
            decay = jnp.broadcast_to(decay_ref[pl.ds(n, 1), cols], (8, LANES))
            end = xs[0]
            for j in range(1, BLOCK):
                end = end * decay + xs[j]
            ends_ref[pl.ds(g * 8 * pitch + n, 8, stride=pitch), cols] = end
        return carry

    lax.fori_loop(0, rows // span, group, 0)


def scan_blocks(blocks, ends_ref, step_ref, modes, cols, start, out_ref=None):
    pitch = ends_ref.shape[0] // blocks
    groups = modes // 8
    steps = [step_ref[pl.ds(i * 8, 8), cols] for i in range(groups)]
    outs = [out_ref[pl.ds(i * 8, 8), cols] for i in range(groups)] if out_ref is not None else None
    states = list(start)
    for b in range(blocks):
        for i in range(groups):
            where = pl.ds(b * pitch + i * 8, 8)
            end = ends_ref[where, cols]
            if outs is not None:
                ends_ref[where, cols] = states[i] * outs[i]
            states[i] = states[i] * steps[i] + end
    return states


def respond(x_ref, hidden_ref, ends_ref, powers_ref, kernel_ref, result_ref, modes, cols):
    rows = x_ref.shape[0]
    blocks = rows // BLOCK
    span = 8 * BLOCK
    pitch = ends_ref.shape[0] // blocks

    def group(g, carry):
        base = pl.multiple_of(g * span, span)
        coefs = [ends_ref[pl.ds(g * 8 * pitch + n, 8, stride=pitch), cols] for n in range(modes)]
        xs = [x_ref[pl.ds(base + j, 8, stride=BLOCK), cols] for j in range(BLOCK)]
        for j in range(BLOCK):
            power = jnp.broadcast_to(powers_ref[pl.ds(j, 1), cols], (8, LANES))
            total = coefs[modes - 1]
            for n in range(modes - 2, -1, -1):
                total = total * power + coefs[n]
            total = total * power
            for i in range(j + 1):
                total = total + xs[i] * jnp.broadcast_to(
                    kernel_ref[pl.ds(j - i, 1), cols], (8, LANES)
                )
            where = pl.ds(base + j, 8, stride=BLOCK)
            gelu = 0.5 * total * (1.0 + lax.erf(total * 0.7071067811865476))
            result_ref[where, cols] = hidden_ref[where, cols] + gelu
        return carry

    lax.fori_loop(0, rows // span, group, 0)


MESH = pl.DeviceIdType.MESH


def pool_kernel(highs, coarse_ref, weight_ref, hidden_ref, all_ref, cols_ref, sems):
    part, place = lax.axis_index("parts"), lax.axis_index("tm")
    high, low = place // SPLIT, place % SPLIT
    depth, width = weight_ref.shape[0], cols_ref.shape[1]
    half = depth // 2
    rows = coarse_ref.shape[0]
    piece = rows // PIECES
    chunk = SPLIT * depth
    other = 1 - part
    (near_send, near_recv, own_sem, line_send, line_recv, side_send, side_recv,
     rows_send, rows_recv) = sems
    flip = lambda bit: low + bit - 2 * bit * ((low // bit) % 2)
    core, cross = flip(1), flip(2)
    diagonal = SPLIT - 1 - low
    at = lambda p, h, l: (p, h * SPLIT + l)

    barrier = pltpu.get_barrier_semaphore()

    def greet(device):
        pl.semaphore_signal(barrier, inc=1, device_id=device, device_id_type=MESH)

    for who in (core, cross, diagonal):
        greet(at(part, high, who))
    greet(at(other, high, low))
    pl.when(high > 0)(lambda: greet(at(part, high - 1, low)))
    pl.when(high < highs - 1)(lambda: greet(at(part, high + 1, low)))

    def spot(h, l, which):
        start = pl.multiple_of(h * chunk + l * depth + which * half, half)
        return cols_ref.at[pl.ds(start, half), :]

    def near(bit, which):
        to = (core, cross, diagonal)[bit]
        mine = weight_ref.at[
            pl.ds(pl.multiple_of(which * half, half), half),
            pl.ds(pl.multiple_of(to * width, width), width),
        ]
        return pltpu.make_async_remote_copy(
            mine, spot(high, low, which), near_send.at[bit, which], near_recv.at[bit, which],
            device_id=at(part, high, to), device_id_type=MESH,
        )

    def near_arrived(bit, which):
        who = (core, cross, diagonal)[bit]
        pltpu.make_async_remote_copy(
            spot(high, who, which), spot(high, who, which), near_send.at[bit, which],
            near_recv.at[bit, which], device_id=at(part, high, who), device_id_type=MESH,
        ).wait_recv()

    def line(up, h, l):
        to = jnp.clip(high + (1 if up else -1), 0, highs - 1)
        return pltpu.make_async_remote_copy(
            spot(h, l, part), spot(h, l, part), line_send.at[int(up), h, l], line_recv.at[h, l],
            device_id=at(part, to, low), device_id_type=MESH,
        )

    def side(h, l, which):
        return pltpu.make_async_remote_copy(
            spot(h, l, which), spot(h, l, which), side_send.at[h, l], side_recv.at[h, l],
            device_id=at(other, high, low), device_id_type=MESH,
        )

    def block(owner, p):
        start = pl.multiple_of(owner * rows + p * piece, piece)
        return all_ref.at[pl.ds(start, piece), :]

    def give(bit, p):
        to = core if bit == 0 else cross
        return pltpu.make_async_remote_copy(
            coarse_ref.at[pl.ds(p * piece, piece), :], block(low, p), rows_send.at[bit, p],
            rows_recv.at[bit, p], device_id=at(part, high, to), device_id_type=MESH,
        )

    def taken(bit, p):
        who = (core, cross, diagonal)[bit]
        pltpu.make_async_remote_copy(
            block(who, p), block(who, p), rows_send.at[bit, p], rows_recv.at[bit, p],
            device_id=at(part, high, core), device_id_type=MESH,
        ).wait_recv()

    def pass_on(p):
        return pltpu.make_async_remote_copy(
            block(cross, p), block(cross, p), rows_send.at[2, p], rows_recv.at[2, p],
            device_id=at(part, high, core), device_id_type=MESH,
        )

    own_weight = pltpu.make_async_copy(
        weight_ref.at[:, pl.ds(pl.multiple_of(low * width, width), width)],
        cols_ref.at[pl.ds(pl.multiple_of(high * chunk + low * depth, depth), depth), :],
        own_sem.at[0],
    )
    own_rows = pltpu.make_async_copy(
        coarse_ref, all_ref.at[pl.ds(pl.multiple_of(low * rows, rows), rows), :], own_sem.at[1]
    )
    own_weight.start()
    own_rows.start()
    ahead = jnp.minimum(high, 1) + jnp.minimum(highs - 1 - high, 1)
    pl.semaphore_wait(barrier, 4 + ahead)

    for bit in (1, 2, 0):
        near(bit, part).start()
    for p in range(PIECES):
        give(1, p).start()
    for p in range(PIECES):
        give(0, p).start()
    for bit in (1, 2, 0):
        near(bit, other).start()

    def both_ways(h, l):
        pl.when(high < highs - 1)(lambda: line(True, h, l).start())
        pl.when(high > 0)(lambda: line(False, h, l).start())

    own_weight.wait()
    both_ways(high, low)
    for bit, who in ((0, core), (1, cross), (2, diagonal)):
        near_arrived(bit, part)
        both_ways(high, who)

    def relay(s, l):
        @pl.when(high - s >= 0)
        def _():
            h = high - s
            line(True, h, l).wait_recv()
            pl.when(high < highs - 1)(lambda: line(True, h, l).start())
            side(h, l, part).start()

        @pl.when(high + s < highs)
        def _():
            h = high + s
            line(False, h, l).wait_recv()
            pl.when(high > 0)(lambda: line(False, h, l).start())
            side(h, l, part).start()

    def step(s, carry):
        for l in range(SPLIT):
            relay(s, l)

        @pl.when(s < PIECES)
        def _():
            taken(1, s - 1)
            pass_on(s - 1).start()

        return carry

    last = highs - 1
    lax.fori_loop(1, last, step, 0)
    for l in range(SPLIT - 1):
        relay(last, l)
    for p in range(min(PIECES - 1, last - 1), PIECES):
        taken(1, p)
        pass_on(p).start()
    own_rows.wait()
    for p in range(PIECES):
        taken(0, p)
        taken(2, p)
    for bit in range(3):
        near_arrived(bit, other)

    def multiply(h):
        start = pl.multiple_of(h * chunk, chunk)
        return jnp.dot(
            all_ref[:, pl.ds(start, chunk)], cols_ref[pl.ds(start, chunk), :],
            preferred_element_type=jnp.float32,
        )

    def keep(value, first):
        for g in range(width // LANES):
            piece_of = value[:, g * LANES : (g + 1) * LANES]
            hidden_ref[g] = piece_of if first else hidden_ref[g] + piece_of

    keep(multiply(high), True)

    def add(s, carry):
        for h, there in ((high - s, high - s >= 0), (high + s, high + s < highs)):
            @pl.when(there)
            def _(h=h):
                for l in range(SPLIT):
                    side(h, l, other).wait_recv()
                keep(multiply(h), False)

        return carry

    lax.fori_loop(1, last, add, 0)
    relay(last, SPLIT - 1)
    add(last, 0)

    for bit in range(3):
        near(bit, 0).wait_send()
        near(bit, 1).wait_send()
    for p in range(PIECES):
        give(0, p).wait_send()
        give(1, p).wait_send()
        pass_on(p).wait_send()

    def sent(h, carry):
        for l in range(SPLIT):
            pl.when((h <= high) & (high < highs - 1))(lambda: line(True, h, l).wait_send())
            pl.when((h >= high) & (high > 0))(lambda: line(False, h, l).wait_send())
            pl.when(h != high)(lambda: side(h, l, part).wait_send())
        return carry

    lax.fori_loop(0, highs, sent, 0)


def pool(coarse, weight):
    rows, features = coarse.shape
    width = weight.shape[1] // SPLIT
    highs = lax.axis_size("tm") // SPLIT
    dma = pltpu.SemaphoreType.DMA
    vmem = pl.BlockSpec(memory_space=pltpu.VMEM)
    return pl.pallas_call(
        functools.partial(pool_kernel, highs),
        out_shape=jax.ShapeDtypeStruct((width // LANES, rows * SPLIT, LANES), jnp.float32),
        in_specs=[vmem, vmem],
        out_specs=vmem,
        scratch_shapes=[
            pltpu.VMEM((rows * SPLIT, features), jnp.bfloat16),
            pltpu.VMEM((features, width), jnp.bfloat16),
            [
                dma((3, 2)), dma((3, 2)), dma((2,)), dma((2, highs, SPLIT)), dma((highs, SPLIT)),
                dma((highs, SPLIT)), dma((highs, SPLIT)), dma((3, PIECES)), dma((3, PIECES)),
            ],
        ],
        compiler_params=pltpu.CompilerParams(collective_id=0, has_side_effects=True),
    )(coarse, weight)


def tables(step_row, out_mix, skip_row, rows):
    modes = out_mix.shape[0]
    rates = step_row[None, :] * (jnp.arange(modes, dtype=jnp.float32) + 1.0)[:, None]
    in_scale = jnp.sqrt(-jnp.expm1(-2.0 * rates))
    out = out_mix * in_scale
    lags = jnp.arange(BLOCK, dtype=jnp.float32)
    kernel = jnp.sum(out[None] * jnp.exp(-lags[:, None, None] * rates[None]), axis=1)
    kernel = kernel.at[0].add(skip_row)
    powers = jnp.exp(-(lags + 1.0)[:, None] * step_row[None, :])
    return jnp.concatenate(
        [jnp.exp(-rates), jnp.exp(-rates * BLOCK), jnp.exp(-rates * rows), out]
        + [jnp.pad(extra, ((0, modes - BLOCK), (0, 0))) for extra in (powers, kernel)]
    )


def layers_kernel(
    highs, modes, hidden_in_ref, gain_ref, table_ref, out_ref, hidden_ref, x_ref, ends_ref,
    stats_ref, last_ref, states_ref, rounded_ref, sems
):
    stats_send, stats_recv, state_send, state_recv, out_send, out_recv = sems
    part, place = lax.axis_index("parts"), lax.axis_index("tm")
    high, low = place // SPLIT, place % SPLIT
    groups, rows, _ = hidden_in_ref.shape
    chans = groups * LANES
    layers = gain_ref.shape[0]
    flip = lambda bit: low + bit - 2 * bit * ((low // bit) % 2)
    near = (flip(1), flip(2), SPLIT - 1 - low)
    at = lambda h, l: (part, h * SPLIT + l)
    own_rows = rows // SPLIT
    blocks = rows // BLOCK
    exact = lax.Precision.HIGHEST

    barrier = pltpu.get_barrier_semaphore()

    def greet(device):
        pl.semaphore_signal(barrier, inc=1, device_id=device, device_id_type=MESH)

    for who in near:
        greet(at(high, who))

    def greet_high(h, carry):
        pl.when(h != high)(lambda: greet(at(h, low)))
        return carry

    lax.fori_loop(0, highs, greet_high, 0)

    def stats_copy(l, bit, owner):
        return pltpu.make_async_remote_copy(
            stats_ref.at[l, owner], stats_ref.at[l, owner], stats_send.at[l, bit],
            stats_recv.at[l, bit], device_id=at(high, near[bit]), device_id_type=MESH,
        )

    def state_copy(l, g, source, target):
        return pltpu.make_async_remote_copy(
            last_ref.at[l, g], states_ref.at[l, source, g], state_send.at[l, target, g],
            state_recv.at[l, source, g], device_id=at(target, low), device_id_type=MESH,
        )

    def out_cols(owner, g):
        return pl.ds(pl.multiple_of(owner * chans + g * LANES, LANES), LANES)

    def out_copy(g, bit, owner):
        start = pl.multiple_of(near[bit] * own_rows, own_rows)
        return pltpu.make_async_remote_copy(
            rounded_ref.at[g, pl.ds(start, own_rows), :], out_ref.at[:, out_cols(owner, g)],
            out_send.at[g, bit], out_recv.at[g, bit],
            device_id=at(high, near[bit]), device_id_type=MESH,
        )

    for l in range(layers):
        source_ref = hidden_in_ref if l == 0 else hidden_ref
        total = source_ref[0]
        for g in range(1, groups):
            total = total + source_ref[g]
        mean = jnp.sum(total, axis=-1, keepdims=True) / chans
        square = jnp.square(source_ref[0] - mean)
        for g in range(1, groups):
            square = square + jnp.square(source_ref[g] - mean)
        ones = jnp.ones((8, LANES), jnp.float32)
        across = lambda v: lax.dot_general(
            ones, v, (((1,), (1,)), ((), ())), precision=exact, preferred_element_type=jnp.float32
        )
        line = lax.broadcasted_iota(jnp.int32, (8, rows), 0)
        stats_ref[l, low] = jnp.where(line == 0, across(total) / chans, across(square))
        if l == 0:
            pl.semaphore_wait(barrier, 3 + highs - 1)
        for bit in (1, 2, 0):
            stats_copy(l, bit, low).start()
        for bit in range(3):
            stats_copy(l, bit, near[bit]).wait_recv()
        every = [stats_ref[l, i] for i in range(SPLIT)]
        means = [e[0:1] for e in every]
        row_mean = (means[0] + means[1] + means[2] + means[3]) / SPLIT
        row_var = sum(e[1:2] + chans * jnp.square(e[0:1] - row_mean) for e in every)
        row_scale = lax.rsqrt(row_var / (chans * SPLIT) + 1e-05)
        both = jnp.where(line == 0, row_mean, row_scale)
        both = jnp.transpose(both)
        row_mean, row_scale = both[:, 0:1], both[:, 1:2]
        for g in range(groups):
            gain = gain_ref[pl.ds(l, 1), pl.ds(g * LANES, LANES)]
            x_ref[g] = (source_ref[g] - row_mean) * row_scale * gain

        def table(index, g, size):
            return table_ref.at[l, pl.ds(index * modes, size), pl.ds(pl.multiple_of(g * LANES, LANES), LANES)]

        cols = slice(None)
        eights = modes // 8

        def send(g):
            def one(h, carry):
                pl.when(h > high)(lambda: state_copy(l, g, high, h).start())
                return carry

            lax.fori_loop(1, highs, one, 0)

        def ends(g, carry):
            block_ends(x_ref.at[g], table(0, g, modes), ends_ref.at[g], modes, cols)
            zero = [jnp.zeros((8, LANES), jnp.float32)] * eights
            last = scan_blocks(blocks, ends_ref.at[g], table(1, g, modes), modes, cols, zero)
            for i in range(eights):
                last_ref[l, g, pl.ds(i * 8, 8), :] = last[i]
            send(g)
            return carry

        lax.fori_loop(0, groups, ends, 0)

        def finish(g, carry):
            whole = table(2, g, modes)

            def join(h, start):
                @pl.when(h < high)
                def _():
                    state_copy(l, g, h, high).wait_recv()
                    states_ref[l, high, g] = whole[...] * states_ref[l, high, g] + states_ref[l, h, g]
                return start

            states_ref[l, high, g] = jnp.zeros((modes, LANES), jnp.float32)
            lax.fori_loop(0, highs - 1, join, 0)
            start = [states_ref[l, high, g, pl.ds(i * 8, 8), :] for i in range(eights)]
            scan_blocks(
                blocks, ends_ref.at[g], table(1, g, modes), modes, cols, start, table(3, g, modes)
            )
            respond(
                x_ref.at[g], source_ref.at[g], ends_ref.at[g], table(4, g, BLOCK),
                table(5, g, BLOCK), hidden_ref.at[g], modes, cols,
            )
            if l == layers - 1:
                rounded_ref[g] = hidden_ref[g].astype(jnp.bfloat16)
                for bit in (1, 2, 0):
                    out_copy(g, bit, low).start()
                out_ref[:, out_cols(low, g)] = rounded_ref[
                    g, pl.ds(pl.multiple_of(low * own_rows, own_rows), own_rows), :
                ]
            return carry

        lax.fori_loop(0, groups, finish, 0)

    def drain(g, carry):
        for bit in range(3):
            out_copy(g, bit, near[bit]).wait_recv()
            out_copy(g, bit, low).wait_send()

        def one(h, carry):
            @pl.when(h > high)
            def _():
                for l in range(layers):
                    state_copy(l, g, high, h).wait_send()
            return carry

        return lax.fori_loop(1, highs, one, carry)

    lax.fori_loop(0, groups, drain, 0)
    for l in range(layers):
        for bit in range(3):
            stats_copy(l, bit, low).wait_send()


def run_layers(hidden, gain, table, modes):
    groups, rows, _ = hidden.shape
    layers = gain.shape[0]
    highs = lax.axis_size("tm") // SPLIT
    dma = pltpu.SemaphoreType.DMA
    vmem = pl.BlockSpec(memory_space=pltpu.VMEM)
    f32 = jnp.float32
    return pl.pallas_call(
        functools.partial(layers_kernel, highs, modes),
        out_shape=jax.ShapeDtypeStruct((rows // SPLIT, groups * LANES * SPLIT), jnp.bfloat16),
        in_specs=[vmem] * 3,
        out_specs=vmem,
        scratch_shapes=[
            pltpu.VMEM((groups, rows, LANES), f32),
            pltpu.VMEM((groups, rows, LANES), f32),
            pltpu.VMEM((groups, (modes + PAD) * (rows // BLOCK), LANES), f32),
            pltpu.VMEM((layers, SPLIT, 8, rows), f32),
            pltpu.VMEM((layers, groups, modes, LANES), f32),
            pltpu.VMEM((layers, highs, groups, modes, LANES), f32),
            pltpu.VMEM((groups, rows, LANES), jnp.bfloat16),
            [
                dma((layers, 3)), dma((layers, 3)), dma((layers, highs, groups)),
                dma((layers, highs, groups)), dma((groups, 3)), dma((groups, 3)),
            ],
        ],
        compiler_params=pltpu.CompilerParams(collective_id=1, has_side_effects=True),
    )(hidden, gain, table)


def local(signal, pool_weight, norm_gain, step_size, mode_out, skip_gain):
    fine_rows, channels = signal.shape
    low = lax.axis_index("tm") % SPLIT
    coarse = signal.reshape(fine_rows // POOL, POOL * channels)
    chans = pool_weight.shape[1] // SPLIT
    rows = SPLIT * coarse.shape[0]
    modes = mode_out.shape[1]

    def own(array):
        return lax.dynamic_slice_in_dim(array, low * chans, chans, axis=array.ndim - 1)

    gain, step, mix, skip = own(norm_gain), own(step_size), own(mode_out), own(skip_gain)
    table = jax.vmap(functools.partial(tables, rows=rows))(step, mix, skip)
    hidden = pool(coarse, pool_weight)
    return run_layers(hidden, gain, table, modes)


def solution(mesh):
    placed = (P(("parts", "tm"), None), P("tm", None), P(), P(), P(), P())
    return jax.shard_map(
        local, mesh=mesh, in_specs=placed, out_specs=P(("parts", "tm"), None), check_vma=False
    )
```
